768 devices in a mesh: blk: 16 (over y, z_hi), dev: 48 (over x, z_lo, core).
Axes of the slice: x: 4, y: 8, z: 12 (z_hi: 2, z_lo: 6; z = z_hi * 6 + z_lo), core: 2. Of those that a mesh axis runs over, the one named last changes fastest.
Arguments:
- factors: bfloat16 [393216, 128], P(('blk', 'dev')), may hold values from -3 to 3
- item_factors: bfloat16 [2048, 128], P('blk')
- block_values: bfloat16 [73728, 128, 128], P(('blk', 'dev')), may hold values from 0 to 8, as said below
- block_rows: int32 [73728], P(('blk', 'dev')), may hold values from 0 to 191, as said below
- block_cols: int32 [73728], P(('blk', 'dev')), may hold values from -1 to 15, as said below
- row_place: int32 [16, 192], P('blk'), may hold values from 0 to 191, as said below
Outputs:
- solution: float32 [393216, 128], P(('blk', 'dev'))
- residual: float32 [393216, 128], P(('blk', 'dev'))
The draws below stay inside these ranges and needn't reach their ends.
Inputs may be any that keep to these rules, and one draw needn't show every extreme that they name: `row_place`: each row of the table is a permutation of 0 to 191: user block row g of the group is held by the device value // 4 of dev, at block position value % 4. `block_rows`: slots 2 o and 2 o + 1 of a device's list hold blocks of user block rows held by device o of dev in the same blk group, whether live or not. `block_cols`: empty slots are marked -1 and their values are to be ignored. Of the two slots that one device holds for one holder device, at most one is live. No two live blocks share both user block row and item block. Of the slots bound for one holder device, at most 3 live ones fall on one item block, and in every blk group some device receives exactly 3 live blocks on every item block. `block_values`: entries are zero or between 0.5 and 8.
All inputs are finite; a program needn't handle non-finite values.
Results may differ from the reference program's by a relative error of at most 0.0054.
Values may be sent and summed in bfloat16 or wider, within the bound.
No kernel may reach another device: no remote copies, remote signals or barrier semaphores. Data moves between devices by JAX's collectives and lax.ppermute only.
A program may use at most 32 MiB of HBM per device.

```python
import math
import jax
import jax.numpy as jnp
from jax import lax

RANK = 128
BS = 128
UB = 4
ITERS = 2
GROUP_ROWS = 192
USERS = 393216
ITEMS = 2048
SLOTS = 73728
N_BLK = 16
N_DEV = 48


def shared_layout(key):
    group_rows = UB * N_DEV
    place_keys = jax.random.split(jax.random.fold_in(key, 101), N_BLK)
    placement = jax.vmap(lambda sub: jax.random.permutation(sub, group_rows))(place_keys).astype(jnp.int32)
    inverse = jnp.argsort(placement, axis=1).astype(jnp.int32)
    order_keys = jax.random.split(jax.random.fold_in(key, 102), N_BLK * N_DEV)
    orders = jax.vmap(lambda sub: jax.random.permutation(sub, N_DEV))(order_keys).astype(jnp.int32)
    orders = orders.reshape(N_BLK, N_DEV, N_DEV)
    panel = orders % N_BLK
    within = orders // N_BLK
    offsets = jax.random.randint(jax.random.fold_in(key, 103), (N_BLK, N_DEV, N_BLK), 0, UB).astype(jnp.int32)
    shifted = jnp.take_along_axis(offsets, panel, axis=2)
    local_row = (within + shifted) % UB
    holder = jnp.arange(N_DEV, dtype=jnp.int32)[None, :, None]
    held_position = (holder * UB + local_row).reshape(N_BLK, N_DEV * N_DEV)
    group_row = jnp.take_along_axis(inverse, held_position, axis=1).reshape(N_BLK, N_DEV, N_DEV)
    shifts = jax.random.randint(jax.random.fold_in(key, 104), (N_BLK, N_DEV), 0, 4).astype(jnp.int32)
    levels = jnp.right_shift(jnp.full((N_BLK, N_DEV), N_DEV, jnp.int32), shifts)
    full_holder = jax.random.randint(jax.random.fold_in(key, 105), (N_BLK, 1), 0, N_DEV).astype(jnp.int32)
    levels = jnp.where(jnp.arange(N_DEV, dtype=jnp.int32)[None, :] == full_holder, N_DEV, levels)
    tickets = jax.random.randint(jax.random.fold_in(key, 106), (N_BLK, N_DEV, N_DEV), 0, N_DEV).astype(jnp.int32)
    is_live = tickets < levels[:, :, None]
    item_col = jnp.where(is_live, panel, -1)
    rows_pair = jnp.transpose(group_row, (0, 2, 1)).astype(jnp.int32)
    cols_pair = jnp.transpose(item_col, (0, 2, 1)).astype(jnp.int32)
    side = jax.random.randint(jax.random.fold_in(key, 107), (N_BLK, N_DEV, N_DEV), 0, 2).astype(jnp.int32)
    first_col = jnp.where(side == 0, cols_pair, -1)
    second_col = jnp.where(side == 1, cols_pair, -1)
    cols_out = jnp.stack([first_col, second_col], axis=-1).reshape(-1).astype(jnp.int32)
    rows_out = jnp.stack([rows_pair, rows_pair], axis=-1).reshape(-1).astype(jnp.int32)
    return (placement, rows_out, cols_out)


def draw_row_place(key, part):
    return shared_layout(key)[0]


def draw_block_rows(key, part):
    return shared_layout(key)[1]


def draw_block_cols(key, part):
    return shared_layout(key)[2]


def draw_block_values(key, part):
    shape = (SLOTS, BS, BS)
    present = jax.random.randint(jax.random.fold_in(key, 201), shape, 0, 5) < 2
    exponent = jax.random.uniform(jax.random.fold_in(key, 202), shape, jnp.float32, 0.0, math.log(16.0))
    magnitude = 0.5 * jnp.exp(exponent)
    return jnp.where(present, magnitude, 0.0).astype(jnp.bfloat16)


def draw_item_factors(key, part):
    row_scale = jnp.exp(jax.random.uniform(jax.random.fold_in(key, 301), (ITEMS, 1), jnp.float32, 0.0, math.log(10.0)))
    col_scale = jnp.exp(jax.random.uniform(jax.random.fold_in(key, 302), (1, RANK), jnp.float32, 0.0, math.log(10.0)))
    base = jax.random.normal(jax.random.fold_in(key, 303), (ITEMS, RANK), jnp.float32)
    return (base * row_scale * col_scale / (21.5 * math.sqrt(ITEMS))).astype(jnp.bfloat16)


def steps_of(rng, shape, shards, low, top_value):
    gain, own = 1.0, jax.random.fold_in(rng, 6)
    for position, shards_of in shards:
        heights = jnp.exp(jax.random.uniform(jax.random.fold_in(own, position), (shards_of,), jnp.float32, low / len(shards), top_value / len(shards)))
        gain = gain * jnp.repeat(heights, shape[position] // shards_of).reshape([-1 if axis == position else 1 for axis in range(len(shape))])
    return gain


def scatter_about(key, dims, deviation, reach, cuts=(), kind=jnp.bfloat16):
    factor_of = steps_of(key, dims, cuts, -0.22, 0.18) if cuts else 1.0
    result = jax.random.normal(key, dims, jnp.float32) * deviation * factor_of
    return jnp.minimum(jnp.maximum(result, -reach), reach).astype(kind)


def setup_inputs(seed: int = 0) -> dict:
    key_of = jax.random.split(jax.random.key(seed), 7)
    factors = scatter_about(key_of[0], (USERS, RANK), 0.5, 3.0, ((0, 768),))
    item_factors = draw_item_factors(jax.random.fold_in(key_of[6], 71), 0)
    block_values = draw_block_values(jax.random.fold_in(key_of[6], 71), 0)
    block_rows = draw_block_rows(jax.random.fold_in(key_of[6], 71), 0)
    block_cols = draw_block_cols(jax.random.fold_in(key_of[6], 71), 0)
    row_place = draw_row_place(jax.random.fold_in(key_of[6], 71), 0)
    return dict(factors=factors, item_factors=item_factors, block_values=block_values, block_rows=block_rows, block_cols=block_cols, row_place=row_place)


ridge_weight = 0.5
epsilon = 1e-6


def reference(factors, item_factors, block_values, block_rows, block_cols, row_place):
    gram_matrix = jnp.dot(item_factors.T, item_factors, preferred_element_type=jnp.float32)
    item_panels = item_factors.reshape(N_BLK, BS, RANK).astype(jnp.float32)
    per_group = 2 * N_DEV * N_DEV
    values = block_values.reshape(N_BLK, per_group, BS, BS)
    user_index = block_rows.reshape(N_BLK, per_group).astype(jnp.int32)
    item_index = block_cols.reshape(N_BLK, per_group).astype(jnp.int32)
    positions = jnp.take_along_axis(row_place.astype(jnp.int32), user_index, axis=1).astype(jnp.int32)
    is_live = item_index >= 0
    safe_items = jnp.maximum(item_index, 0).astype(jnp.int32)

    def group_term(direction, with_rhs):
        def one_group(operands):
            group_dir, group_values, group_pos, group_items, group_live = operands
            masked = jnp.where(group_live[:, None, None], group_values, jnp.zeros((), jnp.bfloat16))
            item_rows = item_panels[group_items]
            user_rows = group_dir[group_pos].astype(jnp.float32)
            scores = jnp.einsum("sur,sir->sui", user_rows, item_rows)
            scaled = (scores * masked.astype(jnp.float32)).astype(jnp.bfloat16)
            carried = jnp.einsum("sui,sir->sur", scaled.astype(jnp.float32), item_rows)
            block_sum = jax.ops.segment_sum(carried, group_pos, num_segments=GROUP_ROWS)
            if with_rhs:
                confidence = jnp.where(masked > 0, 1.0 + masked.astype(jnp.float32), 0.0).astype(jnp.bfloat16)
                lifted = jnp.einsum("sui,sir->sur", confidence.astype(jnp.float32), item_rows)
                return block_sum, jax.ops.segment_sum(lifted, group_pos, num_segments=GROUP_ROWS)
            return block_sum

        return lax.map(one_group, (direction, values, positions, safe_items, is_live))

    def operator_rest(vector, block_sum):
        return block_sum.reshape(USERS, RANK) + jnp.dot(vector, gram_matrix, precision=lax.Precision.HIGHEST) + ridge_weight * vector

    solution = factors.astype(jnp.float32)
    first_term, right_side = group_term(factors.reshape(N_BLK, GROUP_ROWS, BS, RANK), True)
    residual = right_side.reshape(USERS, RANK) - operator_rest(solution, first_term)
    direction = residual
    norm_now = jnp.sum(residual * residual, axis=1)
    for sweep_index in range(ITERS):
        block_sum = group_term(direction.astype(jnp.bfloat16).reshape(N_BLK, GROUP_ROWS, BS, RANK), False)
        image = operator_rest(direction, block_sum)
        curvature = jnp.sum(direction * image, axis=1)
        step_length = norm_now / (curvature + epsilon)
        solution = solution + step_length[:, None] * direction
        residual = residual - step_length[:, None] * image
        if sweep_index + 1 < ITERS:
            norm_next = jnp.sum(residual * residual, axis=1)
            direction = residual + (norm_next / (norm_now + epsilon))[:, None] * direction
            norm_now = norm_next
    return solution, residual
```

```python
import jax
import jax.numpy as jnp
from jax import lax
from jax.experimental import pallas as pl
from jax.experimental.pallas import tpu as pltpu
from jax.sharding import PartitionSpec as P

ITERS = 2

ridge_weight = 0.5
epsilon = 1e-06


META_ROWS = 8


def pick_kernel(cols_ref, rows_ref, place_ref, values_ref, out_ref, staged, read_sem, write_sem):
    holders, _, width = out_ref.shape
    edge = values_ref.shape[1]
    user_blocks = place_ref.shape[1] // holders
    panels = lax.axis_size("blk")
    for holder in range(holders):
        second = (cols_ref[2 * holder + 1] >= 0).astype(jnp.int32)
        pltpu.make_async_copy(
            values_ref.at[2 * holder + second], staged.at[holder, pl.ds(0, edge)], read_sem
        ).start()
    for holder in range(holders):
        col = jnp.maximum(cols_ref[2 * holder], cols_ref[2 * holder + 1])
        second = (cols_ref[2 * holder + 1] >= 0).astype(jnp.int32)
        place = place_ref[0, rows_ref[2 * holder + second]] % user_blocks
        code = jnp.where(col >= 0, place * panels + col, -1)
        staged[holder, edge:, :] = jnp.full((META_ROWS, width), code.astype(jnp.float32)).astype(staged.dtype)
    pltpu.make_async_copy(values_ref.at[pl.ds(0, holders)], staged.at[:, pl.ds(0, edge)], read_sem).wait()
    write = pltpu.make_async_copy(staged, out_ref, write_sem)
    write.start()
    write.wait()


def pick_blocks(block_cols, block_rows, row_place, block_values):
    slots, edge, width = block_values.shape
    out = (slots // 2, edge + META_ROWS, width)
    smem = pl.BlockSpec(memory_space=pltpu.SMEM)
    return pl.pallas_call(
        pick_kernel,
        out_shape=jax.ShapeDtypeStruct(out, block_values.dtype),
        in_specs=[smem, smem, smem, pl.BlockSpec(memory_space=pl.ANY)],
        out_specs=pl.BlockSpec(memory_space=pl.ANY),
        scratch_shapes=[
            pltpu.VMEM(out, block_values.dtype),
            pltpu.SemaphoreType.DMA,
            pltpu.SemaphoreType.DMA,
        ],
    )(block_cols, block_rows, row_place, block_values)


def cg_kernel(
    blocks_ref, items_ref, gram_ref, factors_ref, solution_ref, residual_ref,
    weights, meta, codes_vmem, codes_ref, meta_sem, code_sem, sems,
):
    slots = blocks_ref.shape[0]
    edge = blocks_ref.shape[1] - META_ROWS
    items = items_ref.shape[0]
    panels = items // edge
    chunk = 2 * edge

    meta_copy = pltpu.make_async_copy(blocks_ref.at[:, pl.ds(edge, META_ROWS)], meta, meta_sem)
    meta_copy.start()
    weights[...] = jnp.zeros_like(weights)
    meta_copy.wait()
    codes_vmem[...] = jnp.max(meta[...].astype(jnp.float32), axis=1).astype(jnp.int32)
    code_copy = pltpu.make_async_copy(codes_vmem, codes_ref, code_sem)
    code_copy.start()
    code_copy.wait()

    def block_copy(slot):
        code = codes_ref[slot, 0]
        user = pl.multiple_of((code // panels) * edge, edge)
        item = pl.multiple_of((code % panels) * edge, edge)
        return pltpu.make_async_copy(
            blocks_ref.at[slot, pl.ds(0, edge)], weights.at[pl.ds(user, edge), pl.ds(item, edge)], sems.at[slot]
        )

    for slot in range(slots):
        pl.when(codes_ref[slot, 0] >= 0)(lambda slot=slot: block_copy(slot).start())

    def rest(vector):
        return (
            jnp.dot(vector, gram_ref[...], precision=lax.Precision.HIGHEST, preferred_element_type=jnp.float32)
            + ridge_weight * vector
        )

    solution = factors_ref[...].astype(jnp.float32)
    first_rest = rest(solution)

    for slot in range(slots):
        pl.when(codes_ref[slot, 0] >= 0)(lambda slot=slot: block_copy(slot).wait())

    def products(direction, with_rhs):
        total = rhs = None
        for start in range(0, items, chunk):
            rows = items_ref[start : start + chunk, :]
            held = weights[:, start : start + chunk].astype(jnp.float32)
            scores = lax.dot_general(
                direction, rows, (((1,), (1,)), ((), ())), preferred_element_type=jnp.float32
            )
            scaled = (scores * held).astype(jnp.bfloat16)
            part = jnp.dot(scaled, rows, preferred_element_type=jnp.float32)
            total = part if total is None else total + part
            if with_rhs:
                confidence = jnp.where(held > 0, 1.0 + held, 0.0).astype(jnp.bfloat16)
                lifted = jnp.dot(confidence, rows, preferred_element_type=jnp.float32)
                rhs = lifted if rhs is None else rhs + lifted
        return total, rhs

    block_sum, rhs = products(factors_ref[...], True)
    residual = rhs - (block_sum + first_rest)
    direction = residual
    norm_now = jnp.sum(residual * residual, axis=1, keepdims=True)
    for sweep in range(ITERS):
        block_sum, _ = products(direction.astype(jnp.bfloat16), False)
        image = block_sum + rest(direction)
        curvature = jnp.sum(direction * image, axis=1, keepdims=True)
        step_length = norm_now / (curvature + epsilon)
        solution = solution + step_length * direction
        residual = residual - step_length * image
        if sweep + 1 < ITERS:
            norm_next = jnp.sum(residual * residual, axis=1, keepdims=True)
            direction = residual + (norm_next / (norm_now + epsilon)) * direction
            norm_now = norm_next
    solution_ref[...] = solution
    residual_ref[...] = residual


def run_cg(blocks, items, gram, factors):
    users, rank = factors.shape
    slots = blocks.shape[0]
    out = jax.ShapeDtypeStruct((users, rank), jnp.float32)
    vmem = pl.BlockSpec(memory_space=pltpu.VMEM)
    return pl.pallas_call(
        cg_kernel,
        out_shape=(out, out),
        in_specs=[pl.BlockSpec(memory_space=pl.ANY), vmem, vmem, vmem],
        out_specs=(vmem, vmem),
        scratch_shapes=[
            pltpu.VMEM((users, items.shape[0]), blocks.dtype),
            pltpu.VMEM((slots, META_ROWS, rank), blocks.dtype),
            pltpu.VMEM((slots, rank), jnp.int32),
            pltpu.SMEM((slots, rank), jnp.int32),
            pltpu.SemaphoreType.DMA,
            pltpu.SemaphoreType.DMA,
            pltpu.SemaphoreType.DMA((slots,)),
        ],
        compiler_params=pltpu.CompilerParams(vmem_limit_bytes=40 << 20),
    )(blocks, items, gram, factors)


def body(factors, item_factors, block_values, block_rows, block_cols, row_place):
    group_count = lax.axis_size("blk")
    half = lax.axis_index("blk") % 2

    other = lax.ppermute(item_factors, "blk", [(i, i ^ 1) for i in range(group_count)])
    picked = pick_blocks(block_cols, block_rows, row_place, block_values)
    picked, other = lax.optimization_barrier((picked, other))
    blocks = lax.all_to_all(picked, "dev", split_axis=0, concat_axis=0, tiled=True)
    pair = jnp.concatenate(
        [jnp.where(half == 0, item_factors, other), jnp.where(half == 0, other, item_factors)]
    )
    halves = [[2 * i + h for i in range(group_count // 2)] for h in range(2)]
    items = lax.all_gather(pair, "blk", axis=0, tiled=True, axis_index_groups=halves)
    gram = jnp.dot(items.T, items, preferred_element_type=jnp.float32)
    return run_cg(blocks, items, gram, factors)


def solution(mesh):
    return jax.shard_map(
        body,
        mesh=mesh,
        in_specs=(
            P(("blk", "dev"), None),
            P("blk", None),
            P(("blk", "dev"), None, None),
            P(("blk", "dev")),
            P(("blk", "dev")),
            P("blk", None),
        ),
        out_specs=(P(("blk", "dev"), None), P(("blk", "dev"), None)),
        check_vma=False,
    )
```

```python
import jax
import jax.numpy as jnp
from jax import lax
from jax.experimental import pallas as pl
from jax.experimental.pallas import tpu as pltpu
from jax.sharding import PartitionSpec as P

ITERS = 2

ridge_weight = 0.5
epsilon = 1e-06


CHIPS_X, CORES = 4, 2
CHUNK = 512
META_ROWS = 8


def pick_kernel(cols_ref, rows_ref, place_ref, values_ref, out_ref, staged, read_sems, write_sem):
    holders, _, width = out_ref.shape
    edge = values_ref.shape[1]
    user_blocks = place_ref.shape[1] // holders
    panels = lax.axis_size("blk")
    parts = read_sems.shape[0]
    share = holders // parts
    for holder in range(holders):
        second = (cols_ref[2 * holder + 1] >= 0).astype(jnp.int32)
        pltpu.make_async_copy(
            values_ref.at[2 * holder + second],
            staged.at[holder, pl.ds(0, edge)],
            read_sems.at[holder // share],
        ).start()
    for part in range(parts):
        own = pl.ds(part * share, share)
        for holder in range(part * share, (part + 1) * share):
            col = jnp.maximum(cols_ref[2 * holder], cols_ref[2 * holder + 1])
            second = (cols_ref[2 * holder + 1] >= 0).astype(jnp.int32)
            place = place_ref[0, rows_ref[2 * holder + second]] % user_blocks
            code = jnp.where(col >= 0, place * panels + col, -1)
            staged[holder, edge:, :] = jnp.full((META_ROWS, width), code.astype(jnp.float32)).astype(staged.dtype)
        pltpu.make_async_copy(values_ref.at[own], staged.at[own, pl.ds(0, edge)], read_sems.at[part]).wait()
        pltpu.make_async_copy(staged.at[own], out_ref.at[own], write_sem).start()
    pltpu.make_async_copy(staged, out_ref, write_sem).wait()


def pick_blocks(block_cols, block_rows, row_place, block_values):
    slots, edge, width = block_values.shape
    out = (slots // 2, edge + META_ROWS, width)
    smem = pl.BlockSpec(memory_space=pltpu.SMEM)
    return pl.pallas_call(
        pick_kernel,
        out_shape=jax.ShapeDtypeStruct(out, block_values.dtype),
        in_specs=[smem, smem, smem, pl.BlockSpec(memory_space=pl.ANY)],
        out_specs=pl.BlockSpec(memory_space=pl.ANY),
        scratch_shapes=[
            pltpu.VMEM(out, block_values.dtype),
            pltpu.SemaphoreType.DMA((4,)),
            pltpu.SemaphoreType.DMA,
        ],
    )(block_cols, block_rows, row_place, block_values)


def dense_part(vector, gram):
    product = jnp.dot(vector, gram, precision=lax.Precision.HIGHEST, preferred_element_type=jnp.float32)
    return product + ridge_weight * vector


def cg_kernel(
    blocks_ref, items, turned, gram, rest, factors, solution_ref, residual_ref,
    weights, first_scores, meta, codes_vmem, codes, meta_sem, code_sem, block_sems,
):
    slots = blocks_ref.shape[0]
    edge = blocks_ref.shape[1] - META_ROWS
    count = items.shape[0]
    panels = count // edge

    meta_copy = pltpu.make_async_copy(blocks_ref.at[:, pl.ds(edge, META_ROWS)], meta, meta_sem)
    meta_copy.start()
    weights[...] = jnp.zeros_like(weights)
    meta_copy.wait()
    codes_vmem[...] = jnp.max(meta[...].astype(jnp.float32), axis=1).astype(jnp.int32)
    code_copy = pltpu.make_async_copy(codes_vmem, codes, code_sem)
    code_copy.start()
    code_copy.wait()

    def block_copy(slot):
        code = codes[slot, 0]
        user = pl.multiple_of((code // panels) * edge, edge)
        item = pl.multiple_of((code % panels) * edge, edge)
        return pltpu.make_async_copy(
            blocks_ref.at[slot, pl.ds(0, edge)],
            weights.at[pl.ds(user, edge), pl.ds(item, edge)],
            block_sems.at[slot],
        )

    for slot in range(slots):
        pl.when(codes[slot, 0] >= 0)(lambda slot=slot: block_copy(slot).start())

    chunks = [slice(start, start + CHUNK) for start in range(0, count, CHUNK)]

    def scores_of(direction, chunk):
        return jnp.dot(direction, turned[:, chunk], preferred_element_type=jnp.float32)

    for chunk in chunks:
        first_scores[:, chunk] = scores_of(factors[...], chunk)
    for slot in range(slots):
        pl.when(codes[slot, 0] >= 0)(lambda slot=slot: block_copy(slot).wait())

    block_sum = jnp.zeros(factors.shape, jnp.float32)
    rhs = jnp.zeros(factors.shape, jnp.float32)
    for chunk in chunks:
        held = weights[:, chunk].astype(jnp.float32)
        scaled = (first_scores[:, chunk] * held).astype(jnp.bfloat16)
        block_sum += jnp.dot(scaled, items[chunk, :], preferred_element_type=jnp.float32)
        confidence = jnp.where(held > 0, 1.0 + held, 0.0).astype(jnp.bfloat16)
        rhs += jnp.dot(confidence, items[chunk, :], preferred_element_type=jnp.float32)

    solution = factors[...].astype(jnp.float32)
    residual = rhs - (block_sum + rest[...])
    direction = residual
    norm_now = jnp.sum(residual * residual, axis=1, keepdims=True)
    for sweep in range(ITERS):
        rounded = direction.astype(jnp.bfloat16)
        image = dense_part(direction, gram[...])
        for chunk in chunks:
            scaled = (scores_of(rounded, chunk) * weights[:, chunk].astype(jnp.float32)).astype(jnp.bfloat16)
            image += jnp.dot(scaled, items[chunk, :], preferred_element_type=jnp.float32)
        curvature = jnp.sum(direction * image, axis=1, keepdims=True)
        step_length = norm_now / (curvature + epsilon)
        solution = solution + step_length * direction
        residual = residual - step_length * image
        if sweep + 1 < ITERS:
            norm_next = jnp.sum(residual * residual, axis=1, keepdims=True)
            direction = residual + (norm_next / (norm_now + epsilon)) * direction
            norm_now = norm_next
    solution_ref[...] = solution
    residual_ref[...] = residual


def run_cg(blocks, items, turned, gram, first_rest, factors):
    users, rank = factors.shape
    count, slots = items.shape[0], blocks.shape[0]
    out = jax.ShapeDtypeStruct((users, rank), jnp.float32)
    vmem = pl.BlockSpec(memory_space=pltpu.VMEM)
    return pl.pallas_call(
        cg_kernel,
        out_shape=(out, out),
        in_specs=[pl.BlockSpec(memory_space=pl.ANY)] + [vmem] * 5,
        out_specs=(vmem, vmem),
        scratch_shapes=[
            pltpu.VMEM((users, count), blocks.dtype),
            pltpu.VMEM((users, count), jnp.float32),
            pltpu.VMEM((slots, META_ROWS, rank), blocks.dtype),
            pltpu.VMEM((slots, rank), jnp.int32),
            pltpu.SMEM((slots, rank), jnp.int32),
            pltpu.SemaphoreType.DMA,
            pltpu.SemaphoreType.DMA,
            pltpu.SemaphoreType.DMA((slots,)),
        ],
        compiler_params=pltpu.CompilerParams(vmem_limit_bytes=40 << 20),
    )(blocks, items, turned, gram, first_rest, factors)


def border_pairs(group_count, dev_count, depth):
    runs = dev_count // (CHIPS_X * CORES)
    pairs = []
    for group in range(group_count):
        for column in range(CHIPS_X * CORES):
            x, core = divmod(column, CORES)
            for source, target in ((0, runs - 1 - depth), (runs - 1, depth)):
                pairs.append(
                    (
                        group * dev_count + (x * runs + source) * CORES + core,
                        (group ^ 1) * dev_count + (x * runs + target) * CORES + core,
                    )
                )
    return pairs


def from_other_group(block):
    group_count, dev_count = lax.axis_size("blk"), lax.axis_size("dev")
    runs = dev_count // (CHIPS_X * CORES)
    place = (lax.axis_index("dev") // CORES) % runs
    depth = jnp.minimum(place, runs - 1 - place)
    result = None
    for behind in reversed(range(runs // 2)):
        got = lax.ppermute(block, ("blk", "dev"), border_pairs(group_count, dev_count, behind))
        result = got if result is None else jnp.where(depth == behind, got, result)
    return result


def body(factors, item_factors, block_values, block_rows, block_cols, row_place):
    group_count = lax.axis_size("blk")
    half = lax.axis_index("blk") % 2

    other = from_other_group(item_factors)
    picked = pick_blocks(block_cols, block_rows, row_place, block_values)
    blocks = lax.all_to_all(picked, "dev", split_axis=0, concat_axis=0, tiled=True)
    pair = jnp.concatenate(
        [jnp.where(half == 0, item_factors, other), jnp.where(half == 0, other, item_factors)]
    )
    halves = [[2 * i + h for i in range(group_count // 2)] for h in range(2)]
    items = lax.all_gather(pair, "blk", axis=0, tiled=True, axis_index_groups=halves)
    turned = items.T
    gram = jnp.dot(turned, items, preferred_element_type=jnp.float32)
    first_rest = dense_part(factors.astype(jnp.float32), gram)
    return run_cg(blocks, items, turned, gram, first_rest, factors)


def solution(mesh):
    return jax.shard_map(
        body,
        mesh=mesh,
        in_specs=(
            P(("blk", "dev"), None),
            P("blk", None),
            P(("blk", "dev"), None, None),
            P(("blk", "dev")),
            P(("blk", "dev")),
            P("blk", None),
        ),
        out_specs=(P(("blk", "dev"), None), P(("blk", "dev"), None)),
        check_vma=False,
    )
```

```python
import jax
import jax.numpy as jnp
from jax import lax
from jax.experimental import pallas as pl
from jax.experimental.pallas import tpu as pltpu
from jax.sharding import PartitionSpec as P

ITERS = 2

ridge_weight = 0.5
epsilon = 1e-06


CHIPS_X, CORES = 4, 2
CHUNK = 1024
PARTS = 2
META_ROWS = 2


def pick_kernel(cols_ref, rows_ref, place_ref, values_ref, out_ref, staged, read_sems, write_sem):
    holders, _, _, width = out_ref.shape
    pairs = values_ref.shape[1]
    user_blocks = place_ref.shape[1] // holders
    panels = lax.axis_size("blk")
    parts = read_sems.shape[0]
    share = holders // parts
    for holder in range(holders):
        second = (cols_ref[2 * holder + 1] >= 0).astype(jnp.int32)
        pltpu.make_async_copy(
            values_ref.at[2 * holder + second],
            staged.at[holder, pl.ds(0, pairs)],
            read_sems.at[holder // share],
        ).start()
    for part in range(parts):
        own = pl.ds(part * share, share)
        for holder in range(part * share, (part + 1) * share):
            col = jnp.maximum(cols_ref[2 * holder], cols_ref[2 * holder + 1])
            second = (cols_ref[2 * holder + 1] >= 0).astype(jnp.int32)
            place = place_ref[0, rows_ref[2 * holder + second]] % user_blocks
            code = jnp.where(col >= 0, place * panels + col, -1)
            staged[holder, pairs] = jnp.full((META_ROWS, width), code.astype(jnp.float32)).astype(staged.dtype)
        pltpu.make_async_copy(values_ref.at[own], staged.at[own, pl.ds(0, pairs)], read_sems.at[part]).wait()
        pltpu.make_async_copy(staged.at[own], out_ref.at[own], write_sem).start()
    pltpu.make_async_copy(staged, out_ref, write_sem).wait()


def pick_blocks(block_cols, block_rows, row_place, block_values):
    slots, edge, width = block_values.shape
    pairs = edge // META_ROWS
    out = (slots // 2, pairs + 1, META_ROWS, width)
    smem = pl.BlockSpec(memory_space=pltpu.SMEM)
    return pl.pallas_call(
        pick_kernel,
        out_shape=jax.ShapeDtypeStruct(out, block_values.dtype),
        in_specs=[smem, smem, smem, pl.BlockSpec(memory_space=pl.ANY)],
        out_specs=pl.BlockSpec(memory_space=pl.ANY),
        scratch_shapes=[
            pltpu.VMEM(out, block_values.dtype),
            pltpu.SemaphoreType.DMA((4,)),
            pltpu.SemaphoreType.DMA,
        ],
    )(block_cols, block_rows, row_place, block_values.reshape(slots, pairs, META_ROWS, width))


def dense_part(vector, gram):
    product = jnp.dot(vector, gram, precision=lax.Precision.HIGHEST, preferred_element_type=jnp.float32)
    return product + ridge_weight * vector


def cg_kernel(
    blocks_ref, items, turned, gram, rest, factors, solution_ref, residual_ref,
    weights, meta, codes_vmem, codes, meta_sem, code_sem, block_sems,
):
    slots, steps, _, width = blocks_ref.shape
    edge = (steps - 1) * META_ROWS
    blocks_ref = blocks_ref.reshape(slots, steps * META_ROWS, width)
    count = items.shape[0]
    panels = count // edge
    shift = panels.bit_length() - 1
    assert panels == 1 << shift

    meta_copy = pltpu.make_async_copy(blocks_ref.at[:, pl.ds(edge, META_ROWS)], meta, meta_sem)
    meta_copy.start()
    weights[...] = jnp.zeros_like(weights)
    meta_copy.wait()
    codes_vmem[...] = jnp.max(meta[...].astype(jnp.float32), axis=1).astype(jnp.int32)
    code_copy = pltpu.make_async_copy(codes_vmem, codes, code_sem)
    code_copy.start()
    code_copy.wait()

    def block_copy(slot):
        code = codes[slot, 0]
        user = pl.multiple_of(lax.shift_right_logical(code, shift) * edge, edge)
        item = pl.multiple_of((code & (panels - 1)) * edge, edge)
        return pltpu.make_async_copy(
            blocks_ref.at[slot, pl.ds(0, edge)],
            weights.at[pl.ds(user, edge), pl.ds(item, edge)],
            block_sems.at[slot],
        )

    for slot in range(slots):
        pl.when(codes[slot, 0] >= 0)(lambda slot=slot: block_copy(slot).start())

    for slot in range(slots):
        pl.when(codes[slot, 0] >= 0)(lambda slot=slot: block_copy(slot).wait())

    chunks = [slice(start, start + CHUNK) for start in range(0, count, CHUNK)]
    share = factors.shape[0] // PARTS
    parts = [slice(part * share, (part + 1) * share) for part in range(PARTS)]

    def scaled(rounded, held, chunk):
        scores = jnp.dot(rounded, turned[:, chunk], preferred_element_type=jnp.float32)
        return (scores * held).astype(jnp.bfloat16)

    states = []
    for part in parts:
        block_sum = jnp.zeros((share, factors.shape[1]), jnp.float32)
        rhs = block_sum
        for chunk in chunks:
            held = weights[part, chunk].astype(jnp.float32)
            block_sum += jnp.dot(
                scaled(factors[part, :], held, chunk), items[chunk, :], preferred_element_type=jnp.float32
            )
            confidence = jnp.where(held > 0, 1.0 + held, 0.0).astype(jnp.bfloat16)
            rhs += jnp.dot(confidence, items[chunk, :], preferred_element_type=jnp.float32)
        residual = rhs - (block_sum + rest[part, :])
        norm_now = jnp.sum(residual * residual, axis=1, keepdims=True)
        states.append((factors[part, :].astype(jnp.float32), residual, residual, norm_now))

    for sweep in range(ITERS):
        for index, part in enumerate(parts):
            solution, residual, direction, norm_now = states[index]
            rounded = direction.astype(jnp.bfloat16)
            image = dense_part(direction, gram[...])
            for chunk in chunks:
                held = weights[part, chunk].astype(jnp.float32)
                image += jnp.dot(
                    scaled(rounded, held, chunk), items[chunk, :], preferred_element_type=jnp.float32
                )
            curvature = jnp.sum(direction * image, axis=1, keepdims=True)
            step_length = norm_now / (curvature + epsilon)
            solution = solution + step_length * direction
            residual = residual - step_length * image
            if sweep + 1 < ITERS:
                norm_next = jnp.sum(residual * residual, axis=1, keepdims=True)
                direction = residual + (norm_next / (norm_now + epsilon)) * direction
                norm_now = norm_next
                states[index] = (solution, residual, direction, norm_now)
            else:
                solution_ref[part, :] = solution
                residual_ref[part, :] = residual


def run_cg(blocks, items, turned, gram, first_rest, factors):
    users, rank = factors.shape
    count, slots = items.shape[0], blocks.shape[0]
    out = jax.ShapeDtypeStruct((users, rank), jnp.float32)
    vmem = pl.BlockSpec(memory_space=pltpu.VMEM)
    return pl.pallas_call(
        cg_kernel,
        out_shape=(out, out),
        in_specs=[pl.BlockSpec(memory_space=pl.ANY)] + [vmem] * 5,
        out_specs=(vmem, vmem),
        scratch_shapes=[
            pltpu.VMEM((users, count), blocks.dtype),
            pltpu.VMEM((slots, META_ROWS, rank), blocks.dtype),
            pltpu.VMEM((slots, rank), jnp.int32),
            pltpu.SMEM((slots, rank), jnp.int32),
            pltpu.SemaphoreType.DMA,
            pltpu.SemaphoreType.DMA,
            pltpu.SemaphoreType.DMA((slots,)),
        ],
        compiler_params=pltpu.CompilerParams(vmem_limit_bytes=40 << 20),
    )(blocks, items, turned, gram, first_rest, factors)


def border_pairs(group_count, dev_count, depth):
    runs = dev_count // (CHIPS_X * CORES)
    pairs = []
    for group in range(group_count):
        for column in range(CHIPS_X * CORES):
            x, core = divmod(column, CORES)
            for source, target in ((0, runs - 1 - depth), (runs - 1, depth)):
                pairs.append(
                    (
                        group * dev_count + (x * runs + source) * CORES + core,
                        (group ^ 1) * dev_count + (x * runs + target) * CORES + core,
                    )
                )
    return pairs


def from_other_group(block):
    group_count, dev_count = lax.axis_size("blk"), lax.axis_size("dev")
    runs = dev_count // (CHIPS_X * CORES)
    place = (lax.axis_index("dev") // CORES) % runs
    depth = jnp.minimum(place, runs - 1 - place)
    result = None
    for behind in reversed(range(runs // 2)):
        got = lax.ppermute(block, ("blk", "dev"), border_pairs(group_count, dev_count, behind))
        result = got if result is None else jnp.where(depth == behind, got, result)
    return result


def body(factors, item_factors, block_values, block_rows, block_cols, row_place):
    group_count = lax.axis_size("blk")
    half = lax.axis_index("blk") % 2

    other = from_other_group(item_factors)
    picked = pick_blocks(block_cols, block_rows, row_place, block_values)
    blocks = lax.all_to_all(picked, "dev", split_axis=0, concat_axis=0, tiled=True)
    pair = jnp.concatenate(
        [jnp.where(half == 0, item_factors, other), jnp.where(half == 0, other, item_factors)]
    )
    halves = [[2 * i + h for i in range(group_count // 2)] for h in range(2)]
    items = lax.all_gather(pair, "blk", axis=0, tiled=True, axis_index_groups=halves)
    turned = items.T
    gram = jnp.dot(turned, items, preferred_element_type=jnp.float32)
    first_rest = dense_part(factors.astype(jnp.float32), gram)
    return run_cg(blocks, items, turned, gram, first_rest, factors)


def solution(mesh):
    return jax.shard_map(
        body,
        mesh=mesh,
        in_specs=(
            P(("blk", "dev"), None),
            P("blk", None),
            P(("blk", "dev"), None, None),
            P(("blk", "dev")),
            P(("blk", "dev")),
            P("blk", None),
        ),
        out_specs=(P(("blk", "dev"), None), P(("blk", "dev"), None)),
        check_vma=False,
    )
```

```python
import jax
import jax.numpy as jnp
from jax import lax
from jax.experimental import pallas as pl
from jax.experimental.pallas import tpu as pltpu
from jax.sharding import PartitionSpec as P

ITERS = 2

ridge_weight = 0.5
epsilon = 1e-06


CHIPS_X, CORES = 4, 2
CHUNK = 1024
PARTS = 2
META_ROWS = 2


def pick_kernel(cols_ref, rows_ref, place_ref, values_ref, out_ref, staged, read_sems, write_sem):
    holders, _, _, width = out_ref.shape
    pairs = values_ref.shape[1]
    user_blocks = place_ref.shape[1] // holders
    panels = lax.axis_size("blk")
    parts = read_sems.shape[0]
    share = holders // parts
    for holder in range(holders):
        second = (cols_ref[2 * holder + 1] >= 0).astype(jnp.int32)
        pltpu.make_async_copy(
            values_ref.at[2 * holder + second],
            staged.at[holder, pl.ds(0, pairs)],
            read_sems.at[holder // share],
        ).start()
    for part in range(parts):
        own = pl.ds(part * share, share)
        for holder in range(part * share, (part + 1) * share):
            col = jnp.maximum(cols_ref[2 * holder], cols_ref[2 * holder + 1])
            second = (cols_ref[2 * holder + 1] >= 0).astype(jnp.int32)
            place = place_ref[0, rows_ref[2 * holder + second]] % user_blocks
            code = jnp.where(col >= 0, place * panels + col, -1)
            staged[holder, pairs] = jnp.full((META_ROWS, width), code.astype(jnp.float32)).astype(staged.dtype)
        pltpu.make_async_copy(values_ref.at[own], staged.at[own, pl.ds(0, pairs)], read_sems.at[part]).wait()
        pltpu.make_async_copy(staged.at[own], out_ref.at[own], write_sem).start()
    pltpu.make_async_copy(staged, out_ref, write_sem).wait()


def pick_blocks(block_cols, block_rows, row_place, block_values):
    slots, edge, width = block_values.shape
    pairs = edge // META_ROWS
    out = (slots // 2, pairs + 1, META_ROWS, width)
    smem = pl.BlockSpec(memory_space=pltpu.SMEM)
    return pl.pallas_call(
        pick_kernel,
        out_shape=jax.ShapeDtypeStruct(out, block_values.dtype),
        in_specs=[smem, smem, smem, pl.BlockSpec(memory_space=pl.ANY)],
        out_specs=pl.BlockSpec(memory_space=pl.ANY),
        scratch_shapes=[
            pltpu.VMEM(out, block_values.dtype),
            pltpu.SemaphoreType.DMA((8,)),
            pltpu.SemaphoreType.DMA,
        ],
    )(block_cols, block_rows, row_place, block_values.reshape(slots, pairs, META_ROWS, width))


def dense_part(vector, gram):
    product = jnp.dot(vector, gram, precision=lax.Precision.HIGHEST, preferred_element_type=jnp.float32)
    return product + ridge_weight * vector


def cg_kernel(
    blocks_ref, items, turned, gram, rest, factors, solution_ref, residual_ref,
    weights, codes_vmem, codes, code_sem, block_sems,
):
    slots, steps, _, width = blocks_ref.shape
    edge = (steps - 1) * META_ROWS
    meta = blocks_ref[:, steps - 1]
    blocks = blocks_ref.reshape(slots, steps * META_ROWS, width)
    count = items.shape[0]
    panels = count // edge
    shift = panels.bit_length() - 1
    assert panels == 1 << shift

    codes_vmem[...] = jnp.max(meta.astype(jnp.float32), axis=1).astype(jnp.int32)
    code_copy = pltpu.make_async_copy(codes_vmem, codes, code_sem)
    code_copy.start()
    weights[...] = jnp.zeros_like(weights)
    code_copy.wait()

    def block_copy(slot):
        code = codes[slot, 0]
        user = pl.multiple_of(lax.shift_right_logical(code, shift) * edge, edge)
        item = pl.multiple_of((code & (panels - 1)) * edge, edge)
        return pltpu.make_async_copy(
            blocks.at[slot, pl.ds(0, edge)],
            weights.at[pl.ds(user, edge), pl.ds(item, edge)],
            block_sems.at[slot],
        )

    for slot in range(slots):
        pl.when(codes[slot, 0] >= 0)(lambda slot=slot: block_copy(slot).start())

    for slot in range(slots):
        pl.when(codes[slot, 0] >= 0)(lambda slot=slot: block_copy(slot).wait())

    chunks = [slice(start, start + CHUNK) for start in range(0, count, CHUNK)]
    share = factors.shape[0] // PARTS
    parts = [slice(part * share, (part + 1) * share) for part in range(PARTS)]

    def scaled(rounded, held, chunk):
        scores = jnp.dot(rounded, turned[:, chunk], preferred_element_type=jnp.float32)
        return (scores * held).astype(jnp.bfloat16)

    states = []
    for part in parts:
        block_sum = jnp.zeros((share, factors.shape[1]), jnp.float32)
        rhs = block_sum
        for chunk in chunks:
            held = weights[part, chunk].astype(jnp.float32)
            block_sum += jnp.dot(
                scaled(factors[part, :], held, chunk), items[chunk, :], preferred_element_type=jnp.float32
            )
            confidence = jnp.where(held > 0, 1.0 + held, 0.0).astype(jnp.bfloat16)
            rhs += jnp.dot(confidence, items[chunk, :], preferred_element_type=jnp.float32)
        residual = rhs - (block_sum + rest[part, :])
        norm_now = jnp.sum(residual * residual, axis=1, keepdims=True)
        states.append((factors[part, :].astype(jnp.float32), residual, residual, norm_now))

    for sweep in range(ITERS):
        for index, part in enumerate(parts):
            solution, residual, direction, norm_now = states[index]
            rounded = direction.astype(jnp.bfloat16)
            image = dense_part(direction, gram[...])
            for chunk in chunks:
                held = weights[part, chunk].astype(jnp.float32)
                image += jnp.dot(
                    scaled(rounded, held, chunk), items[chunk, :], preferred_element_type=jnp.float32
                )
            curvature = jnp.sum(direction * image, axis=1, keepdims=True)
            step_length = norm_now / (curvature + epsilon)
            solution = solution + step_length * direction
            residual = residual - step_length * image
            if sweep + 1 < ITERS:
                norm_next = jnp.sum(residual * residual, axis=1, keepdims=True)
                direction = residual + (norm_next / (norm_now + epsilon)) * direction
                norm_now = norm_next
                states[index] = (solution, residual, direction, norm_now)
            else:
                solution_ref[part, :] = solution
                residual_ref[part, :] = residual


def run_cg(blocks, items, turned, gram, first_rest, factors):
    users, rank = factors.shape
    count, slots = items.shape[0], blocks.shape[0]
    out = jax.ShapeDtypeStruct((users, rank), jnp.float32)
    vmem = pl.BlockSpec(memory_space=pltpu.VMEM)
    return pl.pallas_call(
        cg_kernel,
        out_shape=(out, out),
        in_specs=[vmem] * 6,
        out_specs=(vmem, vmem),
        scratch_shapes=[
            pltpu.VMEM((users, count), blocks.dtype),
            pltpu.VMEM((slots, rank), jnp.int32),
            pltpu.SMEM((slots, rank), jnp.int32),
            pltpu.SemaphoreType.DMA,
            pltpu.SemaphoreType.DMA((slots,)),
        ],
        compiler_params=pltpu.CompilerParams(vmem_limit_bytes=40 << 20),
    )(blocks, items, turned, gram, first_rest, factors)


def border_pairs(group_count, dev_count, depth):
    runs = dev_count // (CHIPS_X * CORES)
    pairs = []
    for group in range(group_count):
        for column in range(CHIPS_X * CORES):
            x, core = divmod(column, CORES)
            for source, target in ((0, runs - 1 - depth), (runs - 1, depth)):
                pairs.append(
                    (
                        group * dev_count + (x * runs + source) * CORES + core,
                        (group ^ 1) * dev_count + (x * runs + target) * CORES + core,
                    )
                )
    return pairs


def from_other_group(block):
    group_count, dev_count = lax.axis_size("blk"), lax.axis_size("dev")
    runs = dev_count // (CHIPS_X * CORES)
    place = (lax.axis_index("dev") // CORES) % runs
    depth = jnp.minimum(place, runs - 1 - place)
    result = None
    for behind in reversed(range(runs // 2)):
        got = lax.ppermute(block, ("blk", "dev"), border_pairs(group_count, dev_count, behind))
        result = got if result is None else jnp.where(depth == behind, got, result)
    return result


def body(factors, item_factors, block_values, block_rows, block_cols, row_place):
    group_count = lax.axis_size("blk")
    half = lax.axis_index("blk") % 2

    other = from_other_group(item_factors)
    picked = pick_blocks(block_cols, block_rows, row_place, block_values)
    blocks = lax.all_to_all(picked, "dev", split_axis=0, concat_axis=0, tiled=True)
    pair = jnp.concatenate(
        [jnp.where(half == 0, item_factors, other), jnp.where(half == 0, other, item_factors)]
    )
    halves = [[2 * i + h for i in range(group_count // 2)] for h in range(2)]
    items = lax.all_gather(pair, "blk", axis=0, tiled=True, axis_index_groups=halves)
    turned = items.T
    gram = jnp.dot(turned, items, preferred_element_type=jnp.float32)
    first_rest = dense_part(factors.astype(jnp.float32), gram)
    return run_cg(blocks, items, turned, gram, first_rest, factors)


def solution(mesh):
    return jax.shard_map(
        body,
        mesh=mesh,
        in_specs=(
            P(("blk", "dev"), None),
            P("blk", None),
            P(("blk", "dev"), None, None),
            P(("blk", "dev")),
            P(("blk", "dev")),
            P("blk", None),
        ),
        out_specs=(P(("blk", "dev"), None), P(("blk", "dev"), None)),
        check_vma=False,
    )
```
